256 devices in a mesh: sub: 32 (over x, z), col: 8 (over y, core).
Axes of the slice: x: 4, y: 4, z: 8, core: 2. Of those that a mesh axis runs over, the one named last changes fastest.
Arguments:
- trace_start: bfloat16 [32, 8, 1536, 128], P('sub', 'col'), may hold values from -6 to 6
- neumann_load: bfloat16 [32, 8, 1536, 128], P('sub', 'col'), may hold values from -6 to 6
- double_layer: bfloat16 [32, 8, 1536, 1536], P('sub', 'col'), may hold values from -0.15625 to 0.15625
- single_inverse: bfloat16 [32, 8, 1536, 1536], P('sub', 'col'), may hold values from -0.15625 to 0.15625
- interface_nodes: int32 [32, 8, 8, 128], P('sub', 'col'), may hold values from -1 to 1023, as said below
- node_mode: int32 [32, 8, 1536], P('sub', 'col'), may hold values from 0 to 63
- mode_weight: bfloat16 [32, 8, 1536], P('sub', 'col'), may hold values from 0.5 to 1.5
- coarse_inverse: bfloat16 [16384, 16384], P('sub', 'col'), may hold values from -0.005859375 to 0.005859375
Outputs:
- final_trace: bfloat16 [32, 8, 1536, 128], P('sub', 'col')
- final_residual: bfloat16 [32, 8, 1536, 128], P('sub', 'col')
The draws below stay inside these ranges and needn't reach their ends.
Inputs may be any that keep to these rules, and one draw needn't show every extreme that they name: `interface_nodes`: entry k of block (s, d) is a boundary node of s, within nodes d * 128 to (d + 1) * 128 - 1, distinct within the block, and matches entry k of the neighbour's block for direction 7 - d; valid entries come first and the rest are -1; blocks toward outside the grid are all -1; blocks of directions 1, 3, 4, 6 have 128 / 2 to 128 valid entries, the others 1 to 16, and some block has 128.
All inputs are finite; a program needn't handle non-finite values.
Results may differ from the reference program's by a relative error of at most 0.019.
Values may be sent and summed in bfloat16 or wider, within the bound.
A program may use at most 64 MiB of HBM per device.

```python
import jax
import jax.numpy as jnp
import numpy as np
from jax import lax

M = 1536
R = 128
MODES = 64
IFACE = 128
ITERS = 3
GX = 32
GY = 8
NC = 16384


DIRECTIONS = ((-1, -1), (-1, 0), (-1, 1), (0, -1), (0, 1), (1, -1), (1, 0), (1, 1))


def draw_interface_nodes(key, part):
    face_len = jax.random.randint(jax.random.fold_in(key, 11), (GX, GY, 8), IFACE // 2, IFACE + 1)
    corner_len = jax.random.randint(jax.random.fold_in(key, 37), (GX, GY, 8), 1, IFACE // 8 + 1)
    corner_table = np.array([abs(pair[0]) + abs(pair[1]) == 2 for pair in DIRECTIONS])
    edge_len = jnp.where(jnp.asarray(corner_table)[None, None, :], corner_len, face_len)
    edge_len = edge_len.at[0, 0, 4].set(IFACE)
    row_index = jnp.arange(GX)[:, None]
    col_index = jnp.arange(GY)[None, :]
    lengths = []
    for toward in range(8):
        row_step, col_step = DIRECTIONS[toward]
        inside = (row_index + row_step >= 0) & (row_index + row_step < GX) & (col_index + col_step >= 0) & (col_index + col_step < GY)
        if toward >= 4:
            owner_len = edge_len[:, :, toward]
        else:
            owner_len = jnp.roll(edge_len[:, :, 7 - toward], (-row_step, -col_step), axis=(0, 1))
        lengths.append(jnp.where(inside, owner_len, 0))
    length_all = jnp.stack(lengths, axis=2)
    shuffled = jax.random.permutation(jax.random.fold_in(key, 23), jnp.broadcast_to(jnp.arange(IFACE, dtype=jnp.int32), (GX, GY, 8, IFACE)), axis=-1, independent=True)
    node_ids = jnp.arange(8, dtype=jnp.int32)[:, None] * IFACE + shuffled
    position = jnp.arange(IFACE, dtype=jnp.int32)
    return jnp.where(position < length_all[..., None], node_ids, -1).astype(jnp.int32)


def set_ends(result, rng, low, largest):
    shape = result.shape
    place = [jax.random.randint(jax.random.fold_in(rng, axis), (), 0, shape[axis]) for axis in range(len(shape))]
    result = result.at[tuple(place)].set(low)
    longest = shape.index(max(shape))
    place[longest] = (place[longest] + 1) % shape[longest]
    return result.at[tuple(place)].set(largest)


def block_levels(own_key, extent, cuts, low, high):
    def one(dim, blocks):
        draws = jax.random.uniform(jax.random.fold_in(jax.random.fold_in(own_key, 6), dim), (blocks,), jnp.float32, low / len(cuts), high / len(cuts))
        return jnp.repeat(jnp.exp(draws), extent[dim] // blocks).reshape((-1,) + (1,) * (len(extent) - dim - 1))

    factor_of = one(*cuts[0])
    for cut in cuts[1:]:
        factor_of = factor_of * one(*cut)
    return factor_of


def centred(own_key, shape, scale, most, pieces=(), kind=jnp.bfloat16):
    loudness = block_levels(own_key, shape, pieces, -0.22, 0.18) if pieces else 1.0
    values = jax.random.normal(own_key, shape, jnp.float32) * scale * loudness
    return jnp.minimum(jnp.maximum(values, -most), most).astype(kind)


def setup_inputs(seed: int = 0) -> dict:
    streams_of = jax.random.split(jax.random.key(seed), 9)
    return {
        "trace_start": centred(streams_of[0], (GX, GY, M, R), 1.0, 6.0, ((0, 32), (1, 8))),
        "neumann_load": centred(streams_of[1], (GX, GY, M, R), 1.0, 6.0, ((0, 32), (1, 8))),
        "double_layer": centred(streams_of[2], (GX, GY, M, M), M ** -0.5, 0.15625, ((0, 32), (1, 8))),
        "single_inverse": centred(streams_of[3], (GX, GY, M, M), M ** -0.5, 0.15625, ((0, 32), (1, 8))),
        "interface_nodes": draw_interface_nodes(jax.random.fold_in(streams_of[8], 71), 0),
        "node_mode": set_ends(jax.random.randint(streams_of[5], (GX, GY, M), 0, MODES), jax.random.fold_in(streams_of[5], 1), 0, MODES - 1).astype(jnp.int32),
        "mode_weight": jnp.clip(0.5 + 1.0 * jax.random.uniform(streams_of[6], (GX, GY, M), jnp.float32) ** block_levels(streams_of[6], (GX, GY, M), ((0, 32), (1, 8)), -0.2, 0.2), 0.5, 1.5).astype(jnp.bfloat16),
        "coarse_inverse": centred(streams_of[7], (NC, NC), ((64 * NC) ** -0.5), 0.005859375, ((0, 32), (1, 8))),
    }


DIRECTIONS = ((-1, -1), (-1, 0), (-1, 1), (0, -1), (0, 1), (1, -1), (1, 0), (1, 1))


def steklov(items):
    kernel, inverse, trace_now = items
    mixed_trace = (0.5 * trace_now.astype(jnp.float32) + jnp.dot(kernel, trace_now, preferred_element_type=jnp.float32)).astype(jnp.bfloat16)
    return jnp.dot(inverse, mixed_trace, preferred_element_type=jnp.float32).astype(jnp.bfloat16)


def pick_rows(values, indices):
    return values[indices]


def add_rows(values, indices):
    holder = jnp.zeros((M + 1, R), jnp.float32)
    return holder.at[indices].add(values.astype(jnp.float32))[:M]


def reference(trace_start, neumann_load, double_layer, single_inverse, interface_nodes, node_mode, mode_weight, coarse_inverse):
    flat_kernel = double_layer.reshape(GX * GY, M, M)
    flat_inverse = single_inverse.reshape(GX * GY, M, M)
    valid = (interface_nodes >= 0).reshape(GX, GY, 8 * IFACE)
    safe_index = jnp.where(valid, interface_nodes.reshape(GX, GY, 8 * IFACE), 0).astype(jnp.int32)
    target_index = jnp.where(valid, interface_nodes.reshape(GX, GY, 8 * IFACE), M).astype(jnp.int32)
    mode_range = jnp.arange(MODES, dtype=jnp.int32)
    mode_basis = jnp.where(node_mode[:, :, None, :] == mode_range[None, None, :, None], mode_weight[:, :, None, :], jnp.zeros((), jnp.bfloat16))
    basis_wide = mode_basis.astype(jnp.float32)
    trace_now = trace_start
    residual = trace_start
    for iteration in range(ITERS):
        flux_now = lax.map(steklov, (flat_kernel, flat_inverse, trace_now.reshape(GX * GY, M, R))).reshape(GX, GY, M, R)
        picked = jax.vmap(jax.vmap(pick_rows))(flux_now, safe_index)
        outgoing = jnp.where(valid[..., None], picked, jnp.zeros((), jnp.bfloat16)).reshape(GX, GY, 8, IFACE, R)
        arrivals = []
        for toward in range(8):
            row_step, col_step = DIRECTIONS[toward]
            source = jnp.pad(outgoing[:, :, 7 - toward], ((1, 1), (1, 1), (0, 0), (0, 0)))
            arrivals.append(source[1 + row_step:1 + row_step + GX, 1 + col_step:1 + col_step + GY])
        received = jnp.stack(arrivals, axis=2).reshape(GX, GY, 8 * IFACE, R)
        assembled = flux_now.astype(jnp.float32) + jax.vmap(jax.vmap(add_rows))(received, target_index)
        residual = (neumann_load.astype(jnp.float32) - assembled).astype(jnp.bfloat16)
        residual = lax.optimization_barrier(residual)
        coarse_rhs = jnp.einsum("abmn,abnr->abmr", basis_wide, residual.astype(jnp.float32), precision=lax.Precision.HIGHEST).astype(jnp.bfloat16)
        column_vector = jnp.transpose(coarse_rhs, (1, 0, 2, 3)).reshape(NC, R)
        coarse_out = jnp.dot(coarse_inverse, column_vector, preferred_element_type=jnp.float32).astype(jnp.bfloat16).reshape(GX, GY, MODES, R)
        coarse_out = lax.optimization_barrier(coarse_out)
        correction = jnp.einsum("abmn,abmr->abnr", basis_wide, coarse_out.astype(jnp.float32), precision=lax.Precision.HIGHEST)
        trace_now = (trace_now.astype(jnp.float32) + 0.25 * residual.astype(jnp.float32) + correction).astype(jnp.bfloat16)
    return trace_now, residual
```

```python
import functools

import jax
import jax.numpy as jnp
from jax import lax
from jax.experimental import pallas as pl
from jax.experimental.pallas import tpu as pltpu
from jax.sharding import PartitionSpec as P

MESH = pl.DeviceIdType.MESH
ITERS = 3
M = 1536
R = 128
MODES = 64
XS, ZS = 4, 8
SUB, COL = 32, 8
TILE = 256
TILES = M // TILE
FACES = (1, 3, 4, 6)
CORNERS = (0, 2, 5, 7)
STEPS = ((-1, -1), (-1, 0), (-1, 1), (0, -1), (0, 1), (1, -1), (1, 0), (1, 1))
CSLOTS = 16
ROWS_OUT = 5 * 128
REAL_OUT = 4 * 128 + 4 * CSLOTS
RELAY_UP = (0, 7, 2, 5)
RELAY_DOWN = (1, 6, 3, 4)
Z_ORDER = (4, 3, 5, 2, 6, 1, 7)
BF = jnp.bfloat16
F32 = jnp.float32


def dot(a, b):
    return jnp.dot(a, b, preferred_element_type=F32)


def kernel(
    trace_hbm, load_hbm, k_hbm, s_hbm, iface_ref, mode_ref, weight_ref, c_hbm,
    out_trace, out_resid,
    tv, lv, kv, sv, cv, x_ref, mx, flux, tr, rv, wb, basis,
    sel, sel_t, selc, selc_t, hb, wsel, bw, opart, rhsp, cb, pacc,
    obuf, ebuf, vbuf, pbuf, rbuf,
    in_sem, k_sem, s_sem, out_sem,
    ex_send, ex_recv, ag_send, zr, xr, dr, rs_send, rs_recv,
):
    a = lax.axis_index("sub")
    b = lax.axis_index("col")
    x = a // ZS
    z = a % ZS

    def wrap(i, n):
        return lax.rem(i + n, n)

    barrier = pltpu.get_barrier_semaphore()
    peers = [(wrap(a + STEPS[d][0], SUB), wrap(b + STEPS[d][1], COL)) for d in range(8)]
    greet = list(peers)
    greet += [(x * ZS + wrap(z + dz, ZS), b) for dz in range(1, ZS)]
    greet += [(wrap(x + dx, XS) * ZS + z, b) for dx in (1, -1)]
    greet += [(a, wrap(b + j, COL)) for j in range(1, COL)]
    for peer in greet:
        pl.semaphore_signal(barrier, inc=1, device_id=peer, device_id_type=MESH)

    def rows(i, n):
        return pl.ds(pl.multiple_of(i * n, n), n)

    cp_t = pltpu.make_async_copy(trace_hbm.at[0, 0], tv, in_sem.at[0])
    cp_l = pltpu.make_async_copy(load_hbm.at[0, 0], lv, in_sem.at[1])
    cp_c = pltpu.make_async_copy(c_hbm, cv, in_sem.at[2])

    def k_copy(i):
        return pltpu.make_async_copy(k_hbm.at[0, 0, rows(i, TILE)], kv.at[rows(i, TILE)], k_sem.at[i])

    def s_copy(i):
        return pltpu.make_async_copy(s_hbm.at[0, 0, rows(i, TILE)], sv.at[rows(i, TILE)], s_sem.at[i])

    cp_t.start()
    for i in range(TILES):
        k_copy(i).start()
    for i in range(TILES):
        s_copy(i).start()
    cp_l.start()
    cp_c.start()

    mode_row = mode_ref[0]
    weight_row = weight_ref[0].astype(F32)
    for j in range(M // 128):
        cols = slice(j * 128, (j + 1) * 128)
        part = jnp.where(
            lax.broadcasted_iota(jnp.int32, (128, 128), 0) == mode_row[:, cols],
            weight_row[:, cols],
            0.0,
        )
        basis[:, cols] = part.astype(BF)
        x_ref[cols, 128:] = part.T.astype(BF)

    slots_all = iface_ref[0, 0]
    node_iota = lax.broadcasted_iota(jnp.int32, (128, 128), 0)
    lane_iota = lax.broadcasted_iota(jnp.int32, (128, 128), 1)
    for f, d in enumerate(FACES):
        hot = jnp.where(node_iota == slots_all[d : d + 1] - 128 * d, 1.0, 0.0)
        sel_t[f] = hot.astype(BF)
        sel[f] = hot.T.astype(BF)
    for c, d in enumerate(CORNERS):
        moved = pltpu.roll(slots_all, CSLOTS * c, 1) if c else slots_all
        inside = (lane_iota >= CSLOTS * c) & (lane_iota < CSLOTS * (c + 1))
        hot = jnp.where((node_iota == moved[d : d + 1] - 128 * d) & inside, 1.0, 0.0)
        selc_t[c] = hot.astype(BF)
        selc[c] = hot.T.astype(BF)
    cb[...] = jnp.zeros_like(cb)
    for it in range(ITERS):
        ebuf[it, REAL_OUT:, :] = jnp.zeros((ROWS_OUT - REAL_OUT, R), BF)

    cp_t.wait()
    x_ref[:, :128] = tv[...]
    tr[...] = tv[...].astype(F32)

    def k_tile(i, width):
        span = rows(i, TILE)
        acc = dot(kv[span, :], x_ref[:, :width])
        mx[span, :width] = (acc + 0.5 * x_ref[span, :width].astype(F32)).astype(BF)

    def s_tile_first(i):
        span = rows(i, TILE)
        acc = dot(sv[span, :], mx[...])
        flux[span, :] = acc[:, :128]
        wb[span, :] = acc[:, 128:].astype(BF)

    def s_tile(i):
        span = rows(i, TILE)
        flux[span, :] = dot(sv[span, :], mx[:, :128])

    def band(d):
        return slice(128 * d, 128 * (d + 1))

    def select_from(source):
        pieces = [dot(sel[f], source(band(d))) for f, d in enumerate(FACES)]
        corner = dot(selc[0], source(band(CORNERS[0])))
        for c in range(1, 4):
            corner += dot(selc[c], source(band(CORNERS[c])))
        return pieces + [corner]

    @pl.loop(0, TILES)
    def _(i):
        k_copy(i).wait()
        k_tile(i, 256)

    @pl.loop(0, 4)
    def _(i):
        s_copy(i).wait()
        s_tile_first(i)

    def rhs_of_flux():
        rhsp[...] = dot(basis[...], (lv[...].astype(F32) - flux[...]).astype(BF))

    def send_outgoing(it):
        copies = []
        for d in CORNERS:
            c = CORNERS.index(d)
            there = 512 + CSLOTS * (3 - c)
            here = 512 + CSLOTS * c
            copies.append((peers[d], slice(here, here + CSLOTS), slice(there, there + CSLOTS)))
        for f, d in enumerate(FACES):
            copies.append((peers[d], band(f), band(3 - f)))
        for peer, here, there in copies:
            pltpu.make_async_remote_copy(
                src_ref=obuf.at[it, here], dst_ref=ebuf.at[it, there],
                send_sem=ex_send.at[it], recv_sem=ex_recv.at[it],
                device_id=peer, device_id_type=MESH,
            ).start()

    def wait_bytes(ref, sem):
        pltpu.make_async_copy(ref, ref, sem).wait()

    def slot(ax, az):
        return pl.ds(pl.multiple_of((ax * ZS + az) * MODES, MODES), MODES)

    def send_block(it, where, sem, peer):
        pltpu.make_async_remote_copy(
            src_ref=vbuf.at[it, where], dst_ref=vbuf.at[it, where],
            send_sem=ag_send.at[it], recv_sem=sem, device_id=peer, device_id_type=MESH,
        ).start()

    up = (wrap(x + 1, XS) * ZS + z, b)
    down = (wrap(x - 1, XS) * ZS + z, b)

    def send_z(it):
        own = slot(x, z)
        for dz in Z_ORDER:
            send_block(it, own, zr.at[it, dz - 1], (x * ZS + wrap(z + dz, ZS), b))

    def send_x(it, dz):
        where = slot(x, wrap(z - dz, ZS))
        k_up = RELAY_UP.index(dz) if dz in RELAY_UP else 4
        k_down = RELAY_DOWN.index(dz) if dz in RELAY_DOWN else 4
        send_block(it, where, xr.at[it, 0, k_up], up)
        send_block(it, where, xr.at[it, 1, k_down], down)

    def got_z(it, dz):
        wait_bytes(vbuf.at[it, slot(x, wrap(z - dz, ZS))], zr.at[it, dz - 1])
        send_x(it, dz)

    def relay(it, k):
        where = slot(wrap(x - 1, XS), wrap(z - RELAY_UP[k], ZS))
        wait_bytes(vbuf.at[it, where], xr.at[it, 0, k])
        send_block(it, where, dr.at[it], up)
        where = slot(wrap(x + 1, XS), wrap(z - RELAY_DOWN[k], ZS))
        wait_bytes(vbuf.at[it, where], xr.at[it, 1, k])
        send_block(it, where, dr.at[it], down)

    def coarse_row(it, dx, first):
        span = pl.ds(pl.multiple_of(wrap(x + dx, XS) * (ZS * MODES), ZS * MODES), ZS * MODES)
        part = dot(cv[:, span], vbuf[it, span, :])
        if first:
            pacc[...] = part
        else:
            pacc[...] += part

    def residual_bands(it, group):
        for d in group:
            span = band(d)
            assembled = flux[span, :]
            if d < 8:
                if d in FACES:
                    f = FACES.index(d)
                    assembled += dot(sel_t[f], ebuf[it, band(f), :])
                else:
                    assembled += dot(selc_t[CORNERS.index(d)], ebuf[it, 512:, :])
            resid = (lv[span, :].astype(F32) - assembled).astype(BF)
            rv[span, :] = resid
            moved = tr[span, :] + 0.25 * resid.astype(F32)
            tr[span, :] = moved
            x_ref[span, :128] = moved.astype(BF)

    for it in range(ITERS):
        last = it == ITERS - 1
        if it == 0:
            source = lambda span: flux[span, :].astype(BF)
            for j, piece in enumerate(select_from(source)):
                obuf[it, band(j), :] = piece.astype(BF)
            pl.semaphore_wait(barrier, len(greet))
            send_outgoing(it)

            @pl.loop(4, TILES)
            def _(i):
                s_copy(i).wait()
                s_tile_first(i)

            cp_l.wait()
            cp_c.wait()
            for j, piece in enumerate(select_from(lambda span: wb[span, :])):
                wsel[band(j), :] = piece.astype(BF)
            bw[...] = dot(basis[...], wb[...]).astype(BF)
            for f, d in enumerate(FACES):
                hb[:, band(f)] = dot(basis[:, band(d)], sel_t[f]).astype(BF)
            corner = dot(basis[:, band(CORNERS[0])], selc_t[0])
            for c in range(1, 4):
                corner += dot(basis[:, band(CORNERS[c])], selc_t[c])
            hb[:, 512:] = corner.astype(BF)
            rhs_of_flux()
        else:
            obuf[it] = (opart[...] + dot(wsel[...], cb[...])).astype(BF)
            send_outgoing(it)
            rhsp[...] -= dot(bw[...], cb[...])
            flux[...] += dot(wb[...], cb[...])
            tr[...] += dot(x_ref[:, 128:], cb[...])

        wait_bytes(ebuf.at[it, :REAL_OUT], ex_recv.at[it])
        rhs = rhsp[...] - dot(hb[...], ebuf[it])
        vbuf[it, slot(x, z), :] = rhs[:MODES].astype(BF)
        send_z(it)
        send_x(it, 0)

        jobs = [
            functools.partial(residual_bands, it, range(0, 6)),
            functools.partial(residual_bands, it, range(6, 12)),
        ]
        if not last:
            jobs += [functools.partial(k_tile, i, 128) for i in range(TILES)]
            jobs += [functools.partial(s_tile, i) for i in range(TILES)]

            def finish():
                source = lambda span: flux[span, :].astype(BF)
                for j, piece in enumerate(select_from(source)):
                    opart[band(j), :] = piece
                rhs_of_flux()

            jobs.append(finish)

        def work(n):
            for _ in range(min(n, len(jobs))):
                jobs.pop(0)()

        work(3)
        got_z(it, 1)
        got_z(it, 7)
        relay(it, 0)
        work(2)
        got_z(it, 2)
        got_z(it, 6)
        work(2)
        relay(it, 1)
        got_z(it, 3)
        got_z(it, 5)
        work(1)
        got_z(it, 4)
        coarse_row(it, 0, True)
        relay(it, 2)
        work(2)
        relay(it, 3)
        for side in range(2):
            wait_bytes(vbuf.at[it, : 4 * MODES], xr.at[it, side, 4])
        coarse_row(it, 1, False)
        coarse_row(it, -1, False)
        wait_bytes(vbuf.at[it, : 8 * MODES], dr.at[it])
        coarse_row(it, 2, False)

        pbuf[it] = pacc[...].astype(BF)
        for j in Z_ORDER:
            to = wrap(b + j, COL)
            pltpu.make_async_remote_copy(
                src_ref=pbuf.at[it, rows(to, MODES)], dst_ref=rbuf.at[it, rows(j, MODES)],
                send_sem=rs_send.at[it], recv_sem=rs_recv.at[it],
                device_id=(a, to), device_id_type=MESH,
            ).start()
        if last:
            cp_r = pltpu.make_async_copy(rv, out_resid, out_sem.at[0])
            cp_r.start()
        work(len(jobs))
        wait_bytes(rbuf.at[it, MODES:], rs_recv.at[it])
        total = pacc[rows(b, MODES), :]
        for j in range(1, COL):
            total += rbuf[it, j * MODES : (j + 1) * MODES, :].astype(F32)
        cb[:MODES, :] = total.astype(BF)

    tv[...] = (tr[...] + dot(x_ref[:, 128:], cb[...])).astype(BF)
    cp_o = pltpu.make_async_copy(tv, out_trace, out_sem.at[1])
    cp_o.start()
    for it in range(ITERS):
        wait_bytes(obuf.at[it, :REAL_OUT], ex_send.at[it])
        wait_bytes(vbuf.at[it, : (SUB - 1) * MODES], ag_send.at[it])
        wait_bytes(pbuf.at[it, MODES:], rs_send.at[it])
    cp_r.wait()
    cp_o.wait()


def local(trace_start, neumann_load, double_layer, single_inverse, interface_nodes, node_mode, mode_weight, coarse_inverse):
    hbm = pl.BlockSpec(memory_space=pl.ANY)
    vmem = pl.BlockSpec(memory_space=pltpu.VMEM)
    square = lambda: pltpu.VMEM((M, M), BF)
    tall = lambda kind: pltpu.VMEM((M, R), kind)
    dma = pltpu.SemaphoreType.DMA
    trace, resid = pl.pallas_call(
        kernel,
        out_shape=(jax.ShapeDtypeStruct((M, R), BF), jax.ShapeDtypeStruct((M, R), BF)),
        in_specs=[hbm, hbm, hbm, hbm, vmem, vmem, vmem, hbm],
        out_specs=(hbm, hbm),
        scratch_shapes=[
            tall(BF), tall(BF), square(), square(), pltpu.VMEM((512, 2048), BF),
            pltpu.VMEM((M, 256), BF), pltpu.VMEM((M, 256), BF), tall(F32), tall(F32), tall(BF), tall(BF),
            pltpu.VMEM((128, M), BF),
            pltpu.VMEM((4, 128, 128), BF), pltpu.VMEM((4, 128, 128), BF),
            pltpu.VMEM((4, 128, 128), BF), pltpu.VMEM((4, 128, 128), BF),
            pltpu.VMEM((128, ROWS_OUT), BF), pltpu.VMEM((ROWS_OUT, 128), BF), pltpu.VMEM((128, 128), BF),
            pltpu.VMEM((ROWS_OUT, R), F32), pltpu.VMEM((128, R), F32), pltpu.VMEM((128, R), BF),
            pltpu.VMEM((512, R), F32),
            pltpu.VMEM((ITERS, ROWS_OUT, R), BF), pltpu.VMEM((ITERS, ROWS_OUT, R), BF),
            pltpu.VMEM((ITERS, SUB * MODES, R), BF),
            pltpu.VMEM((ITERS, COL * MODES, R), BF), pltpu.VMEM((ITERS, COL * MODES, R), BF),
            dma((3,)), dma((TILES,)), dma((TILES,)), dma((2,)),
            dma((ITERS,)), dma((ITERS,)), dma((ITERS,)), dma((ITERS, 7)), dma((ITERS, 2, 5)), dma((ITERS,)),
            dma((ITERS,)), dma((ITERS,)),
        ],
        compiler_params=pltpu.CompilerParams(collective_id=0, has_side_effects=True),
    )(trace_start, neumann_load, double_layer, single_inverse, interface_nodes, node_mode, mode_weight, coarse_inverse)
    return trace[None, None], resid[None, None]


def solution(mesh):
    four = P("sub", "col", None, None)
    three = P("sub", "col", None)
    return jax.shard_map(
        local,
        mesh=mesh,
        in_specs=(four, four, four, four, four, three, three, P("sub", "col")),
        out_specs=(four, four),
        check_vma=False,
    )
```

```python
import functools

import jax
import jax.numpy as jnp
from jax import lax
from jax.experimental import pallas as pl
from jax.experimental.pallas import tpu as pltpu
from jax.sharding import PartitionSpec as P

MESH = pl.DeviceIdType.MESH
ITERS = 3
M = 1536
R = 128
MODES = 64
XS, ZS = 4, 8
SUB, COL = 32, 8
TILE = 256
TILES = M // TILE
FACES = (1, 3, 4, 6)
CORNERS = (0, 2, 5, 7)
STEPS = ((-1, -1), (-1, 0), (-1, 1), (0, -1), (0, 1), (1, -1), (1, 0), (1, 1))
CSLOTS = 16
ROWS_OUT = 5 * 128
REAL_OUT = 4 * 128 + 4 * CSLOTS
Z_ORDER = (4, 3, 5, 2, 6, 1, 7)
BF = jnp.bfloat16
F32 = jnp.float32


def dot(a, b):
    return jnp.dot(a, b, preferred_element_type=F32)


def kernel(
    trace_hbm, load_hbm, k_hbm, s_hbm, iface_ref, mode_ref, weight_ref, c_hbm,
    out_trace, out_resid,
    tv, lv, kv, sv, cv, x_ref, mx, flux, tr, wb, basis,
    sel, sel_t, selc, selc_t, hb, wsel, bw, opart, rhsp, cb, pacc,
    obuf, ebuf, vbuf, pbuf, rbuf,
    in_sem, k_sem, s_sem,
    ex_send, ex_recv, ag_send, zr, xr, x_own, zf, rs_send, rs_recv,
):
    a = lax.axis_index("sub")
    b = lax.axis_index("col")
    x = a // ZS
    z = a % ZS

    def wrap(i, n):
        return lax.rem(i + n, n)

    peers = [(wrap(a + STEPS[d][0], SUB), wrap(b + STEPS[d][1], COL)) for d in range(8)]
    greet = list(peers)
    greet += [(x * ZS + wrap(z + dz, ZS), b) for dz in range(1, ZS)]
    greet += [(wrap(x + dx, XS) * ZS + z, b) for dx in range(1, XS)]
    greet += [(a, wrap(b + j, COL)) for j in range(1, COL)]
    def rows(i, n):
        return pl.ds(pl.multiple_of(i * n, n), n)

    cp_t = pltpu.make_async_copy(trace_hbm.at[0, 0], tv, in_sem.at[0])
    cp_l = pltpu.make_async_copy(load_hbm.at[0, 0], lv, in_sem.at[1])
    cp_c = pltpu.make_async_copy(c_hbm, cv, in_sem.at[2])

    def k_copy(i):
        return pltpu.make_async_copy(k_hbm.at[0, 0, rows(i, TILE)], kv.at[rows(i, TILE)], k_sem.at[i])

    def s_copy(i):
        return pltpu.make_async_copy(s_hbm.at[0, 0, rows(i, TILE)], sv.at[rows(i, TILE)], s_sem.at[i])

    cp_t.start()
    for i in range(TILES):
        k_copy(i).start()
    barrier = pltpu.get_barrier_semaphore()
    for peer in greet:
        pl.semaphore_signal(barrier, inc=1, device_id=peer, device_id_type=MESH)

    slots_all = iface_ref[0, 0]
    node_iota = lax.broadcasted_iota(jnp.int32, (128, 128), 0)
    lane_iota = lax.broadcasted_iota(jnp.int32, (128, 128), 1)
    for f, d in enumerate(FACES):
        hot = jnp.where(node_iota == slots_all[d : d + 1] - 128 * d, 1.0, 0.0)
        sel_t[f] = hot.astype(BF)
        sel[f] = hot.T.astype(BF)
    for c, d in enumerate(CORNERS):
        moved = pltpu.roll(slots_all, CSLOTS * c, 1) if c else slots_all
        inside = (lane_iota >= CSLOTS * c) & (lane_iota < CSLOTS * (c + 1))
        hot = jnp.where((node_iota == moved[d : d + 1] - 128 * d) & inside, 1.0, 0.0)
        selc_t[c] = hot.astype(BF)
        selc[c] = hot.T.astype(BF)
    cb[...] = jnp.zeros_like(cb)
    for it in range(ITERS):
        ebuf[it, REAL_OUT:, :] = jnp.zeros((ROWS_OUT - REAL_OUT, R), BF)

    cp_t.wait()
    x_ref[:, :128] = tv[...]
    tr[...] = tv[...].astype(F32)

    def k_tile(i, width, tile=TILE):
        span = rows(i, tile)
        acc = dot(kv[span, :], x_ref[:, :width])
        mx[span, :width] = (acc + 0.5 * x_ref[span, :width].astype(F32)).astype(BF)

    def s_tile_first(i):
        span = rows(i, TILE)
        acc = dot(sv[span, :], mx[...])
        flux[span, :] = acc[:, :128]
        wb[span, :] = acc[:, 128:].astype(BF)

    def s_tile(i, tile=TILE):
        span = rows(i, tile)
        flux[span, :] = dot(sv[span, :], mx[:, :128])

    def band(d):
        return slice(128 * d, 128 * (d + 1))

    def select_from(source):
        pieces = [dot(sel[f], source(band(d))) for f, d in enumerate(FACES)]
        corner = dot(selc[0], source(band(CORNERS[0])))
        for c in range(1, 4):
            corner += dot(selc[c], source(band(CORNERS[c])))
        return pieces + [corner]

    def build_basis():
        mode_row = mode_ref[0]
        weight_row = weight_ref[0].astype(F32)
        for j in range(M // 128):
            cols = slice(j * 128, (j + 1) * 128)
            part = jnp.where(
                lax.broadcasted_iota(jnp.int32, (128, 128), 0) == mode_row[:, cols],
                weight_row[:, cols],
                0.0,
            )
            basis[:, cols] = part.astype(BF)
            x_ref[cols, 128:] = part.T.astype(BF)

    for i in range(TILES):
        s_copy(i).start()
    cp_l.start()
    cp_c.start()
    for i in range(TILES):
        k_copy(i).wait()

    @pl.loop(0, M // 512)
    def _(i):
        k_tile(i, 128, 512)

    for i in range(4):
        s_copy(i).wait()

    @pl.loop(0, 2)
    def _(i):
        s_tile(i, 512)

    def rhs_of_flux():
        rhsp[...] = dot(basis[...], (lv[...].astype(F32) - flux[...]).astype(BF))

    def send_outgoing(it):
        copies = []
        for d in CORNERS:
            c = CORNERS.index(d)
            there = 512 + CSLOTS * (3 - c)
            here = 512 + CSLOTS * c
            copies.append((peers[d], slice(here, here + CSLOTS), slice(there, there + CSLOTS)))
        for f, d in enumerate(FACES):
            copies.append((peers[d], band(f), band(3 - f)))
        for peer, here, there in copies:
            pltpu.make_async_remote_copy(
                src_ref=obuf.at[it, here], dst_ref=ebuf.at[it, there],
                send_sem=ex_send.at[it], recv_sem=ex_recv.at[it],
                device_id=peer, device_id_type=MESH,
            ).start()

    def wait_bytes(ref, sem):
        pltpu.make_async_copy(ref, ref, sem).wait()

    def slot(ax, az):
        return pl.ds(pl.multiple_of((ax * ZS + az) * MODES, MODES), MODES)

    def send_block(it, where, sem, peer):
        pltpu.make_async_remote_copy(
            src_ref=vbuf.at[it, where], dst_ref=vbuf.at[it, where],
            send_sem=ag_send.at[it], recv_sem=sem, device_id=peer, device_id_type=MESH,
        ).start()


    def send_z(it):
        own = slot(x, z)
        for dz in Z_ORDER:
            send_block(it, own, zr.at[it, dz - 1], (x * ZS + wrap(z + dz, ZS), b))

    def send_x(it, dz):
        where = slot(x, wrap(z - dz, ZS))
        sems = x_own if dz == 0 else xr
        for dx in (2, 1, 3):
            send_block(it, where, sems.at[it, dx - 1], (wrap(x + dx, XS) * ZS + z, b))

    def got_z(it, dz):
        wait_bytes(vbuf.at[it, slot(x, wrap(z - dz, ZS))], zr.at[it, dz - 1])
        if dz not in (1, ZS - 1):
            send_x(it, dz)

    def got_own_x(it, dx):
        where = slot(wrap(x - dx, XS), z)
        wait_bytes(vbuf.at[it, where], x_own.at[it, dx - 1])
        for dz in (1, ZS - 1):
            send_block(it, where, zf.at[it, dx - 1], (x * ZS + wrap(z + dz, ZS), b))

    def got_x(it, dx):
        wait_bytes(vbuf.at[it, : 2 * MODES], zf.at[it, dx - 1])
        wait_bytes(vbuf.at[it, : (ZS - 3) * MODES], xr.at[it, dx - 1])
        coarse_row(it, -dx, False)

    def coarse_row(it, dx, first):
        span = pl.ds(pl.multiple_of(wrap(x + dx, XS) * (ZS * MODES), ZS * MODES), ZS * MODES)
        part = dot(cv[:, span], vbuf[it, span, :])
        if first:
            pacc[...] = part
        else:
            pacc[...] += part

    def residual_bands(it, group):
        for d in group:
            span = band(d)
            assembled = flux[span, :]
            if d < 8:
                if d in FACES:
                    f = FACES.index(d)
                    assembled += dot(sel_t[f], ebuf[it, band(f), :])
                else:
                    assembled += dot(selc_t[CORNERS.index(d)], ebuf[it, 512:, :])
            resid = (lv[span, :].astype(F32) - assembled).astype(BF)
            if it == ITERS - 1:
                out_resid[span, :] = resid
            moved = tr[span, :] + 0.25 * resid.astype(F32)
            tr[span, :] = moved
            x_ref[span, :128] = moved.astype(BF)

    for it in range(ITERS):
        last = it == ITERS - 1
        if it == 0:
            source = lambda span: flux[span, :].astype(BF)
            for j, piece in enumerate(select_from(source)):
                obuf[it, band(j), :] = piece.astype(BF)
            pl.semaphore_wait(barrier, len(greet))
            send_outgoing(it)

            for i in range(4, TILES):
                s_copy(i).wait()
            s_tile(2, 512)

            build_basis()
            for f, d in enumerate(FACES):
                hb[:, band(f)] = dot(basis[:, band(d)], sel_t[f]).astype(BF)
            corner = dot(basis[:, band(CORNERS[0])], selc_t[0])
            for c in range(1, 4):
                corner += dot(basis[:, band(CORNERS[c])], selc_t[c])
            hb[:, 512:] = corner.astype(BF)
            cp_l.wait()
            rhs_of_flux()
        else:
            obuf[it] = (opart[...] + dot(wsel[...], cb[...])).astype(BF)
            send_outgoing(it)
            rhsp[...] -= dot(bw[...], cb[...])
            flux[...] += dot(wb[...], cb[...])
            tr[...] += dot(x_ref[:, 128:], cb[...])

        wait_bytes(ebuf.at[it, :REAL_OUT], ex_recv.at[it])
        rhs = rhsp[...] - dot(hb[...], ebuf[it])
        vbuf[it, slot(x, z), :] = rhs[:MODES].astype(BF)
        send_x(it, 0)
        send_z(it)

        jobs = [
            functools.partial(residual_bands, it, range(0, 6)),
            functools.partial(residual_bands, it, range(6, 12)),
        ]
        if not last:
            width, product = (256, s_tile_first) if it == 0 else (128, s_tile)
            jobs += [functools.partial(k_tile, i, width) for i in range(TILES)]
            jobs += [functools.partial(product, i) for i in range(TILES)]

            def finish(it=it):
                if it == 0:
                    for j, piece in enumerate(select_from(lambda span: wb[span, :])):
                        wsel[band(j), :] = piece.astype(BF)
                    bw[...] = dot(basis[...], wb[...]).astype(BF)
                source = lambda span: flux[span, :].astype(BF)
                for j, piece in enumerate(select_from(source)):
                    opart[band(j), :] = piece
                rhs_of_flux()

            jobs.append(finish)

        def work(n):
            for _ in range(min(n, len(jobs))):
                jobs.pop(0)()

        work(6)
        got_own_x(it, 1)
        got_own_x(it, 3)
        got_own_x(it, 2)
        got_z(it, 2)
        got_z(it, 6)
        got_z(it, 3)
        got_z(it, 5)
        got_z(it, 4)
        work(5)
        if it == 0:
            cp_c.wait()
        got_z(it, 1)
        got_z(it, 7)
        coarse_row(it, 0, True)
        got_x(it, 1)
        got_x(it, 3)
        got_x(it, 2)

        pbuf[it] = pacc[...].astype(BF)
        for j in Z_ORDER:
            to = wrap(b + j, COL)
            pltpu.make_async_remote_copy(
                src_ref=pbuf.at[it, rows(to, MODES)], dst_ref=rbuf.at[it, rows(j, MODES)],
                send_sem=rs_send.at[it], recv_sem=rs_recv.at[it],
                device_id=(a, to), device_id_type=MESH,
            ).start()
        work(len(jobs))
        wait_bytes(rbuf.at[it, MODES:], rs_recv.at[it])
        total = pacc[rows(b, MODES), :]
        for j in range(1, COL):
            total += rbuf[it, j * MODES : (j + 1) * MODES, :].astype(F32)
        cb[:MODES, :] = total.astype(BF)

    out_trace[...] = (tr[...] + dot(x_ref[:, 128:], cb[...])).astype(BF)
    for it in range(ITERS):
        wait_bytes(obuf.at[it, :REAL_OUT], ex_send.at[it])
        wait_bytes(vbuf.at[it, : (SUB - 1) * MODES], ag_send.at[it])
        wait_bytes(pbuf.at[it, MODES:], rs_send.at[it])


def store_kernel(trace_ref, resid_ref, out_trace, out_resid, sem):
    first = pltpu.make_async_copy(trace_ref, out_trace.at[0, 0], sem.at[0])
    second = pltpu.make_async_copy(resid_ref, out_resid.at[0, 0], sem.at[1])
    first.start()
    second.start()
    first.wait()
    second.wait()


def local(trace_start, neumann_load, double_layer, single_inverse, interface_nodes, node_mode, mode_weight, coarse_inverse):
    hbm = pl.BlockSpec(memory_space=pl.ANY)
    vmem = pl.BlockSpec(memory_space=pltpu.VMEM)
    square = lambda: pltpu.VMEM((M, M), BF)
    tall = lambda kind: pltpu.VMEM((M, R), kind)
    dma = pltpu.SemaphoreType.DMA
    trace, resid = pl.pallas_call(
        kernel,
        out_shape=(pltpu.VMEM((M, R), BF), pltpu.VMEM((M, R), BF)),
        in_specs=[hbm, hbm, hbm, hbm, vmem, vmem, vmem, hbm],
        out_specs=(vmem, vmem),
        scratch_shapes=[
            tall(BF), tall(BF), square(), square(), pltpu.VMEM((512, 2048), BF),
            pltpu.VMEM((M, 256), BF), pltpu.VMEM((M, 256), BF), tall(F32), tall(F32), tall(BF),
            pltpu.VMEM((128, M), BF),
            pltpu.VMEM((4, 128, 128), BF), pltpu.VMEM((4, 128, 128), BF),
            pltpu.VMEM((4, 128, 128), BF), pltpu.VMEM((4, 128, 128), BF),
            pltpu.VMEM((128, ROWS_OUT), BF), pltpu.VMEM((ROWS_OUT, 128), BF), pltpu.VMEM((128, 128), BF),
            pltpu.VMEM((ROWS_OUT, R), F32), pltpu.VMEM((128, R), F32), pltpu.VMEM((128, R), BF),
            pltpu.VMEM((512, R), F32),
            pltpu.VMEM((ITERS, ROWS_OUT, R), BF), pltpu.VMEM((ITERS, ROWS_OUT, R), BF),
            pltpu.VMEM((ITERS, SUB * MODES, R), BF),
            pltpu.VMEM((ITERS, COL * MODES, R), BF), pltpu.VMEM((ITERS, COL * MODES, R), BF),
            dma((3,)), dma((TILES,)), dma((TILES,)),
            dma((ITERS,)), dma((ITERS,)), dma((ITERS,)), dma((ITERS, 7)), dma((ITERS, 3)), dma((ITERS, 3)), dma((ITERS, 3)),
            dma((ITERS,)), dma((ITERS,)),
        ],
        compiler_params=pltpu.CompilerParams(collective_id=0, has_side_effects=True),
    )(trace_start, neumann_load, double_layer, single_inverse, interface_nodes, node_mode, mode_weight, coarse_inverse)
    return pl.pallas_call(
        store_kernel,
        out_shape=(jax.ShapeDtypeStruct((1, 1, M, R), BF), jax.ShapeDtypeStruct((1, 1, M, R), BF)),
        in_specs=[hbm, hbm],
        out_specs=(hbm, hbm),
        scratch_shapes=[dma((2,))],
        compiler_params=pltpu.CompilerParams(vmem_limit_bytes=1 << 20),
    )(trace, resid)


def solution(mesh):
    four = P("sub", "col", None, None)
    three = P("sub", "col", None)
    return jax.shard_map(
        local,
        mesh=mesh,
        in_specs=(four, four, four, four, four, three, three, P("sub", "col")),
        out_specs=(four, four),
        check_vma=False,
    )
```

```python
import functools

import jax
import jax.numpy as jnp
from jax import lax
from jax.experimental import pallas as pl
from jax.experimental.pallas import tpu as pltpu
from jax.sharding import PartitionSpec as P

MESH = pl.DeviceIdType.MESH
ITERS = 3
M = 1536
R = 128
MODES = 64
XS, ZS = 4, 8
SUB, COL = 32, 8
TILE = 256
TILES = M // TILE
FACES = (1, 3, 4, 6)
CORNERS = (0, 2, 5, 7)
STEPS = ((-1, -1), (-1, 0), (-1, 1), (0, -1), (0, 1), (1, -1), (1, 0), (1, 1))
CSLOTS = 16
ROWS_OUT = 5 * 128
REAL_OUT = 4 * 128 + 4 * CSLOTS
Z_ORDER = (4, 3, 5, 2, 6, 1, 7)
X_ORDER = (1, 3, 2)
X_FIRST = {1: (1, 7), 2: (3, 5, 2, 6, 1, 7), 3: (1, 7)}
BF = jnp.bfloat16
F32 = jnp.float32


def dot(a, b):
    return jnp.dot(a, b, preferred_element_type=F32)


def kernel(
    trace_hbm, load_hbm, k_hbm, s_hbm, iface_ref, mode_ref, weight_ref, c_hbm,
    out_trace, out_resid,
    tv, lv, kv, sv, cv, x_ref, mx, flux, tr, wb, basis,
    sel, sel_t, selc, selc_t, hb, wsel, bw, opart, rhsp, cb, pacc,
    obuf, ebuf, vbuf, pbuf, rbuf,
    in_sem,
    ex_send, ex_recv, ag_send, zr, xr, x_own, rs_send, rs_recv,
):
    a = lax.axis_index("sub")
    b = lax.axis_index("col")
    x = a // ZS
    z = a % ZS
    y = b // 2
    core = b % 2

    def wrap(i, n):
        return lax.rem(i + n, n)

    peers = [(wrap(a + STEPS[d][0], SUB), wrap(b + STEPS[d][1], COL)) for d in range(8)]
    greet = list(peers)
    greet += [(x * ZS + wrap(z + dz, ZS), b) for dz in range(1, ZS)]
    greet += [(wrap(x + dx, XS) * ZS + z, b) for dx in range(1, XS)]
    greet += [(a, wrap(b + j, COL)) for j in range(1, COL)]
    def rows(i, n):
        return pl.ds(pl.multiple_of(i * n, n), n)

    cp_t = pltpu.make_async_copy(trace_hbm.at[0, 0], tv, in_sem.at[0])
    cp_l = pltpu.make_async_copy(load_hbm.at[0, 0], lv, in_sem.at[1])
    cp_c = pltpu.make_async_copy(c_hbm, cv, in_sem.at[2])

    def load_rows(hbm, vmem, first, last, sem):
        span = pl.ds(first, last - first)
        return pltpu.make_async_copy(hbm.at[0, 0, span], vmem.at[span], sem)

    def k_copy(i):
        span = rows(i, 512)
        return pltpu.make_async_copy(k_hbm.at[0, 0, span], kv.at[span], in_sem.at[3 + i])

    s_copies = [load_rows(s_hbm, sv, 0, 1024, in_sem.at[6]), load_rows(s_hbm, sv, 1024, M, in_sem.at[7])]
    cp_t.start()
    k_copy(0).start()

    barrier = pltpu.get_barrier_semaphore()
    for peer in greet:
        pl.semaphore_signal(barrier, inc=1, device_id=peer, device_id_type=MESH)

    slots_all = iface_ref[0, 0]
    node_iota = lax.broadcasted_iota(jnp.int32, (128, 128), 0)
    lane_iota = lax.broadcasted_iota(jnp.int32, (128, 128), 1)
    for f, d in enumerate(FACES):
        hot = jnp.where(node_iota == slots_all[d : d + 1] - 128 * d, 1.0, 0.0)
        sel_t[f] = hot.astype(BF)
        sel[f] = hot.T.astype(BF)
    k_copy(1).start()
    for c, d in enumerate(CORNERS):
        moved = pltpu.roll(slots_all, CSLOTS * c, 1) if c else slots_all
        inside = (lane_iota >= CSLOTS * c) & (lane_iota < CSLOTS * (c + 1))
        hot = jnp.where((node_iota == moved[d : d + 1] - 128 * d) & inside, 1.0, 0.0)
        selc_t[c] = hot.astype(BF)
        selc[c] = hot.T.astype(BF)
    cb[...] = jnp.zeros_like(cb)
    for it in range(ITERS):
        ebuf[it, REAL_OUT:, :] = jnp.zeros((ROWS_OUT - REAL_OUT, R), BF)

    k_copy(2).start()
    for copy in s_copies:
        copy.start()
    cp_l.start()
    cp_c.start()
    cp_t.wait()
    x_ref[:, :128] = tv[...]
    tr[...] = tv[...].astype(F32)

    def k_tile(i, width, tile=TILE):
        span = rows(i, tile)
        acc = dot(kv[span, :], x_ref[:, :width])
        mx[span, :width] = (acc + 0.5 * x_ref[span, :width].astype(F32)).astype(BF)

    def s_tile_first(i):
        span = rows(i, TILE)
        acc = dot(sv[span, :], mx[...])
        flux[span, :] = acc[:, :128]
        wb[span, :] = acc[:, 128:].astype(BF)

    def s_tile(i, tile=TILE):
        span = rows(i, tile)
        flux[span, :] = dot(sv[span, :], mx[:, :128])

    def band(d):
        return slice(128 * d, 128 * (d + 1))

    def select_from(source):
        pieces = [dot(sel[f], source(band(d))) for f, d in enumerate(FACES)]
        corner = dot(selc[0], source(band(CORNERS[0])))
        for c in range(1, 4):
            corner += dot(selc[c], source(band(CORNERS[c])))
        return pieces + [corner]

    def build_basis():
        mode_row = mode_ref[0]
        weight_row = weight_ref[0].astype(F32)
        for j in range(M // 128):
            cols = slice(j * 128, (j + 1) * 128)
            part = jnp.where(
                lax.broadcasted_iota(jnp.int32, (128, 128), 0) == mode_row[:, cols],
                weight_row[:, cols],
                0.0,
            )
            basis[:, cols] = part.astype(BF)
            x_ref[cols, 128:] = part.T.astype(BF)

    @pl.loop(0, 3)
    def _(i):
        k_copy(i).wait()
        k_tile(i, 128, 512)

    s_copies[0].wait()

    @pl.loop(0, 2)
    def _(i):
        s_tile(i, 512)

    def rhs_of_flux():
        rhsp[...] = dot(basis[...], (lv[...].astype(F32) - flux[...]).astype(BF))

    def send_outgoing(it):
        copies = []
        for d in CORNERS:
            c = CORNERS.index(d)
            there = 512 + CSLOTS * (3 - c)
            here = 512 + CSLOTS * c
            copies.append((peers[d], slice(here, here + CSLOTS), slice(there, there + CSLOTS)))
        for f, d in enumerate(FACES):
            copies.append((peers[d], band(f), band(3 - f)))
        for peer, here, there in copies:
            pltpu.make_async_remote_copy(
                src_ref=obuf.at[it, here], dst_ref=ebuf.at[it, there],
                send_sem=ex_send.at[it], recv_sem=ex_recv.at[it],
                device_id=peer, device_id_type=MESH,
            ).start()

    def wait_bytes(ref, sem):
        pltpu.make_async_copy(ref, ref, sem).wait()

    def slot(ax, az):
        return pl.ds(pl.multiple_of((ax * ZS + az) * MODES, MODES), MODES)

    def send_block(it, where, sem, peer):
        pltpu.make_async_remote_copy(
            src_ref=vbuf.at[it, where], dst_ref=vbuf.at[it, where],
            send_sem=ag_send.at[it], recv_sem=sem, device_id=peer, device_id_type=MESH,
        ).start()


    def send_z(it):
        own = slot(x, z)
        for dz in Z_ORDER:
            send_block(it, own, zr.at[it, dz - 1], (x * ZS + wrap(z + dz, ZS), b))

    def send_x(it, dz):
        where = slot(x, wrap(z - dz, ZS))
        sems = x_own if dz == 0 else xr
        for dx in X_ORDER:
            if dz in X_FIRST[dx]:
                continue
            send_block(it, where, sems.at[it, dx - 1], (wrap(x + dx, XS) * ZS + z, b))

    def got_z(it, dz):
        wait_bytes(vbuf.at[it, slot(x, wrap(z - dz, ZS))], zr.at[it, dz - 1])
        send_x(it, dz)

    def got_own_x(it, dx):
        where = slot(wrap(x - dx, XS), z)
        wait_bytes(vbuf.at[it, where], x_own.at[it, dx - 1])
        for dz in X_FIRST[dx]:
            send_block(it, where, xr.at[it, dx - 1], (x * ZS + wrap(z + dz, ZS), b))

    def wait_x(it, dx):
        wait_bytes(vbuf.at[it, : (ZS - 1) * MODES], xr.at[it, dx - 1])

    def got_x(it, dx):
        wait_x(it, dx)
        coarse_row(it, -dx, False)

    def coarse_row(it, dx, first):
        span = pl.ds(pl.multiple_of(wrap(x + dx, XS) * (ZS * MODES), ZS * MODES), ZS * MODES)
        part = dot(cv[:, span], vbuf[it, span, :])
        if first:
            pacc[...] = part
        else:
            pacc[...] += part

    def residual_bands(it, group):
        for d in group:
            span = band(d)
            assembled = flux[span, :]
            if d < 8:
                if d in FACES:
                    f = FACES.index(d)
                    assembled += dot(sel_t[f], ebuf[it, band(f), :])
                else:
                    assembled += dot(selc_t[CORNERS.index(d)], ebuf[it, 512:, :])
            resid = (lv[span, :].astype(F32) - assembled).astype(BF)
            if it == ITERS - 1:
                out_resid[span, :] = resid
            moved = tr[span, :] + 0.25 * resid.astype(F32)
            tr[span, :] = moved
            x_ref[span, :128] = moved.astype(BF)

    for it in range(ITERS):
        last = it == ITERS - 1
        if it == 0:
            source = lambda span: flux[span, :].astype(BF)
            for j, piece in enumerate(select_from(source)):
                obuf[it, band(j), :] = piece.astype(BF)
            pl.semaphore_wait(barrier, len(greet))
            send_outgoing(it)

            s_copies[1].wait()
            s_tile(2, 512)

            build_basis()
            for f, d in enumerate(FACES):
                hb[:, band(f)] = dot(basis[:, band(d)], sel_t[f]).astype(BF)
            corner = dot(basis[:, band(CORNERS[0])], selc_t[0])
            for c in range(1, 4):
                corner += dot(basis[:, band(CORNERS[c])], selc_t[c])
            hb[:, 512:] = corner.astype(BF)
            cp_l.wait()
            rhs_of_flux()
        else:
            obuf[it] = (opart[...] + dot(wsel[...], cb[...])).astype(BF)
            send_outgoing(it)
            rhsp[...] -= dot(bw[...], cb[...])
            flux[...] += dot(wb[...], cb[...])
            tr[...] += dot(x_ref[:, 128:], cb[...])

        wait_bytes(ebuf.at[it, :REAL_OUT], ex_recv.at[it])
        rhs = rhsp[...] - dot(hb[...], ebuf[it])
        vbuf[it, slot(x, z), :] = rhs[:MODES].astype(BF)
        send_x(it, 0)
        send_z(it)

        jobs = [
            functools.partial(residual_bands, it, range(0, 6)),
            functools.partial(residual_bands, it, range(6, 12)),
        ]
        if not last:
            width, product = (256, s_tile_first) if it == 0 else (128, s_tile)
            jobs += [functools.partial(k_tile, i, width) for i in range(TILES)]
            jobs += [functools.partial(product, i) for i in range(TILES)]

            def finish(it=it):
                if it == 0:
                    for j, piece in enumerate(select_from(lambda span: wb[span, :])):
                        wsel[band(j), :] = piece.astype(BF)
                    bw[...] = dot(basis[...], wb[...]).astype(BF)
                source = lambda span: flux[span, :].astype(BF)
                for j, piece in enumerate(select_from(source)):
                    opart[band(j), :] = piece
                rhs_of_flux()

            jobs.append(finish)

        def work(n):
            for _ in range(min(n, len(jobs))):
                jobs.pop(0)()

        work(6)
        got_own_x(it, 1)
        got_own_x(it, 3)
        got_own_x(it, 2)
        got_z(it, 2)
        got_z(it, 6)
        got_z(it, 3)
        got_z(it, 5)
        got_z(it, 4)
        work(5)
        if it == 0:
            cp_c.wait()
        got_z(it, 1)
        got_z(it, 7)
        coarse_row(it, 0, True)
        got_x(it, 1)
        got_x(it, 3)
        got_x(it, 2)

        pbuf[it] = pacc[...].astype(BF)
        for dy, dc in ((2, 0), (2, 1), (1, 0), (3, 0), (1, 1), (3, 1), (0, 1)):
            to = 2 * wrap(y + dy, 4) + wrap(core + dc, 2)
            pltpu.make_async_remote_copy(
                src_ref=pbuf.at[it, rows(to, MODES)], dst_ref=rbuf.at[it, rows(2 * dy + dc, MODES)],
                send_sem=rs_send.at[it], recv_sem=rs_recv.at[it],
                device_id=(a, to), device_id_type=MESH,
            ).start()
        work(len(jobs))
        wait_bytes(rbuf.at[it, MODES:], rs_recv.at[it])
        total = pacc[rows(b, MODES), :]
        for j in range(1, COL):
            total += rbuf[it, j * MODES : (j + 1) * MODES, :].astype(F32)
        cb[:MODES, :] = total.astype(BF)

    out_trace[...] = (tr[...] + dot(x_ref[:, 128:], cb[...])).astype(BF)
    for it in range(ITERS):
        wait_bytes(obuf.at[it, :REAL_OUT], ex_send.at[it])
        wait_bytes(vbuf.at[it, : (SUB - 1) * MODES], ag_send.at[it])
        wait_bytes(pbuf.at[it, MODES:], rs_send.at[it])


def store_kernel(trace_ref, resid_ref, out_trace, out_resid, sem):
    first = pltpu.make_async_copy(trace_ref, out_trace.at[0, 0], sem.at[0])
    second = pltpu.make_async_copy(resid_ref, out_resid.at[0, 0], sem.at[1])
    first.start()
    second.start()
    first.wait()
    second.wait()


def local(trace_start, neumann_load, double_layer, single_inverse, interface_nodes, node_mode, mode_weight, coarse_inverse):
    hbm = pl.BlockSpec(memory_space=pl.ANY)
    vmem = pl.BlockSpec(memory_space=pltpu.VMEM)
    square = lambda: pltpu.VMEM((M, M), BF)
    tall = lambda kind: pltpu.VMEM((M, R), kind)
    dma = pltpu.SemaphoreType.DMA
    trace, resid = pl.pallas_call(
        kernel,
        out_shape=(pltpu.VMEM((M, R), BF), pltpu.VMEM((M, R), BF)),
        in_specs=[hbm, hbm, hbm, hbm, vmem, vmem, vmem, hbm],
        out_specs=(vmem, vmem),
        scratch_shapes=[
            tall(BF), tall(BF), square(), square(), pltpu.VMEM((512, 2048), BF),
            pltpu.VMEM((M, 256), BF), pltpu.VMEM((M, 256), BF), tall(F32), tall(F32), tall(BF),
            pltpu.VMEM((128, M), BF),
            pltpu.VMEM((4, 128, 128), BF), pltpu.VMEM((4, 128, 128), BF),
            pltpu.VMEM((4, 128, 128), BF), pltpu.VMEM((4, 128, 128), BF),
            pltpu.VMEM((128, ROWS_OUT), BF), pltpu.VMEM((ROWS_OUT, 128), BF), pltpu.VMEM((128, 128), BF),
            pltpu.VMEM((ROWS_OUT, R), F32), pltpu.VMEM((128, R), F32), pltpu.VMEM((128, R), BF),
            pltpu.VMEM((512, R), F32),
            pltpu.VMEM((ITERS, ROWS_OUT, R), BF), pltpu.VMEM((ITERS, ROWS_OUT, R), BF),
            pltpu.VMEM((ITERS, SUB * MODES, R), BF),
            pltpu.VMEM((ITERS, COL * MODES, R), BF), pltpu.VMEM((ITERS, COL * MODES, R), BF),
            dma((8,)),
            dma((ITERS,)), dma((ITERS,)), dma((ITERS,)), dma((ITERS, 7)), dma((ITERS, 3)), dma((ITERS, 3)),
            dma((ITERS,)), dma((ITERS,)),
        ],
        compiler_params=pltpu.CompilerParams(collective_id=0, has_side_effects=True),
    )(trace_start, neumann_load, double_layer, single_inverse, interface_nodes, node_mode, mode_weight, coarse_inverse)
    return pl.pallas_call(
        store_kernel,
        out_shape=(jax.ShapeDtypeStruct((1, 1, M, R), BF), jax.ShapeDtypeStruct((1, 1, M, R), BF)),
        in_specs=[hbm, hbm],
        out_specs=(hbm, hbm),
        scratch_shapes=[dma((2,))],
        compiler_params=pltpu.CompilerParams(vmem_limit_bytes=1 << 20),
    )(trace, resid)


def solution(mesh):
    four = P("sub", "col", None, None)
    three = P("sub", "col", None)
    return jax.shard_map(
        local,
        mesh=mesh,
        in_specs=(four, four, four, four, four, three, three, P("sub", "col")),
        out_specs=(four, four),
        check_vma=False,
    )
```

```python
import functools

import jax
import jax.numpy as jnp
from jax import lax
from jax.experimental import pallas as pl
from jax.experimental.pallas import tpu as pltpu
from jax.sharding import PartitionSpec as P

MESH = pl.DeviceIdType.MESH
ITERS = 3
M = 1536
R = 128
MODES = 64
XS, ZS = 4, 8
SUB, COL = 32, 8
TILE = 256
TILES = M // TILE
FACES = (1, 3, 4, 6)
CORNERS = (0, 2, 5, 7)
STEPS = ((-1, -1), (-1, 0), (-1, 1), (0, -1), (0, 1), (1, -1), (1, 0), (1, 1))
CSLOTS = 16
ROWS_OUT = 5 * 128
REAL_OUT = 4 * 128 + 4 * CSLOTS
Z_ORDER = (4, 3, 5, 2, 6, 1, 7)
X_ORDER = (1, 3, 2)
X_FIRST = {1: (1, 7), 2: (3, 5, 2, 6, 1, 7), 3: (1, 7)}
BF = jnp.bfloat16
F32 = jnp.float32


def dot(a, b):
    return jnp.dot(a, b, preferred_element_type=F32)


def kernel(
    trace_hbm, load_hbm, k_hbm, s_hbm, iface_ref, mode_ref, weight_ref, c_hbm,
    out_trace, out_resid,
    tv, lv, kv, sv, cv, x_ref, mx, flux, tr, wb, basis,
    sel, sel_t, selc, selc_t, hb, wsel, bw, opart, rhsp, cb, pacc,
    obuf, ebuf, vbuf, pbuf, rbuf,
    in_sem,
    ex_send, ex_recv, ag_send, zr, xr, x_own, rs_send, rs_recv,
):
    a = lax.axis_index("sub")
    b = lax.axis_index("col")
    x = a // ZS
    z = a % ZS
    y = b // 2
    core = b % 2

    def wrap(i, n):
        return lax.rem(i + n, n)

    peers = [(wrap(a + STEPS[d][0], SUB), wrap(b + STEPS[d][1], COL)) for d in range(8)]
    greet = list(peers)
    greet += [(x * ZS + wrap(z + dz, ZS), b) for dz in range(1, ZS)]
    greet += [(wrap(x + dx, XS) * ZS + z, b) for dx in range(1, XS)]
    greet += [(a, wrap(b + j, COL)) for j in range(1, COL)]
    def rows(i, n):
        return pl.ds(pl.multiple_of(i * n, n), n)

    cp_t = pltpu.make_async_copy(trace_hbm.at[0, 0], tv, in_sem.at[0])
    cp_l = pltpu.make_async_copy(load_hbm.at[0, 0], lv, in_sem.at[1])
    cp_c = pltpu.make_async_copy(c_hbm, cv, in_sem.at[2])

    def k_copy(i):
        span = rows(i, 512)
        return pltpu.make_async_copy(k_hbm.at[0, 0, span], kv.at[span], in_sem.at[3 + i])

    def s_copy(i):
        span = rows(i, 512)
        return pltpu.make_async_copy(s_hbm.at[0, 0, span], sv.at[span], in_sem.at[6 + i])

    cp_t.start()
    k_copy(0).start()

    barrier = pltpu.get_barrier_semaphore()
    for peer in greet:
        pl.semaphore_signal(barrier, inc=1, device_id=peer, device_id_type=MESH)

    slots_all = iface_ref[0, 0]
    node_iota = lax.broadcasted_iota(jnp.int32, (128, 128), 0)
    lane_iota = lax.broadcasted_iota(jnp.int32, (128, 128), 1)
    for f, d in enumerate(FACES):
        hot = jnp.where(node_iota == slots_all[d : d + 1] - 128 * d, 1.0, 0.0)
        sel_t[f] = hot.astype(BF)
        sel[f] = hot.T.astype(BF)
    k_copy(1).start()
    for c, d in enumerate(CORNERS):
        moved = pltpu.roll(slots_all, CSLOTS * c, 1) if c else slots_all
        inside = (lane_iota >= CSLOTS * c) & (lane_iota < CSLOTS * (c + 1))
        hot = jnp.where((node_iota == moved[d : d + 1] - 128 * d) & inside, 1.0, 0.0)
        selc_t[c] = hot.astype(BF)
        selc[c] = hot.T.astype(BF)
    cb[...] = jnp.zeros_like(cb)
    for it in range(ITERS):
        ebuf[it, REAL_OUT:, :] = jnp.zeros((ROWS_OUT - REAL_OUT, R), BF)

    k_copy(2).start()
    for i in range(3):
        s_copy(i).start()
    cp_t.wait()
    x_ref[:, :128] = tv[...]
    tr[...] = tv[...].astype(F32)

    def k_tile(i, width, tile=TILE):
        span = rows(i, tile)
        acc = dot(kv[span, :], x_ref[:, :width])
        mx[span, :width] = (acc + 0.5 * x_ref[span, :width].astype(F32)).astype(BF)

    def s_tile_first(i):
        span = rows(i, TILE)
        acc = dot(sv[span, :], mx[...])
        flux[span, :] = acc[:, :128]
        wb[span, :] = acc[:, 128:].astype(BF)

    def s_tile(i, tile=TILE):
        span = rows(i, tile)
        flux[span, :] = dot(sv[span, :], mx[:, :128])

    def band(d):
        return slice(128 * d, 128 * (d + 1))

    def select_from(source):
        pieces = [dot(sel[f], source(band(d))) for f, d in enumerate(FACES)]
        corner = dot(selc[0], source(band(CORNERS[0])))
        for c in range(1, 4):
            corner += dot(selc[c], source(band(CORNERS[c])))
        return pieces + [corner]

    def build_basis():
        mode_row = mode_ref[0]
        weight_row = weight_ref[0].astype(F32)
        for j in range(M // 128):
            cols = slice(j * 128, (j + 1) * 128)
            part = jnp.where(
                lax.broadcasted_iota(jnp.int32, (128, 128), 0) == mode_row[:, cols],
                weight_row[:, cols],
                0.0,
            )
            basis[:, cols] = part.astype(BF)
            x_ref[cols, 128:] = part.T.astype(BF)

    @pl.loop(0, 3)
    def _(i):
        k_copy(i).wait()
        k_tile(i, 128, 512)

    @pl.loop(0, 2)
    def _(i):
        s_copy(i).wait()
        s_tile(i, 512)

    cp_l.start()
    cp_c.start()

    def rhs_of_flux():
        rhsp[...] = dot(basis[...], (lv[...].astype(F32) - flux[...]).astype(BF))

    def send_outgoing(it):
        copies = []
        for d in CORNERS:
            c = CORNERS.index(d)
            there = 512 + CSLOTS * (3 - c)
            here = 512 + CSLOTS * c
            copies.append((peers[d], slice(here, here + CSLOTS), slice(there, there + CSLOTS)))
        for f, d in enumerate(FACES):
            copies.append((peers[d], band(f), band(3 - f)))
        for peer, here, there in copies:
            pltpu.make_async_remote_copy(
                src_ref=obuf.at[it, here], dst_ref=ebuf.at[it, there],
                send_sem=ex_send.at[it], recv_sem=ex_recv.at[it],
                device_id=peer, device_id_type=MESH,
            ).start()

    def wait_bytes(ref, sem):
        pltpu.make_async_copy(ref, ref, sem).wait()

    def slot(ax, az):
        return pl.ds(pl.multiple_of((ax * ZS + az) * MODES, MODES), MODES)

    def send_block(it, where, sem, peer):
        pltpu.make_async_remote_copy(
            src_ref=vbuf.at[it, where], dst_ref=vbuf.at[it, where],
            send_sem=ag_send.at[it], recv_sem=sem, device_id=peer, device_id_type=MESH,
        ).start()


    def send_z(it):
        own = slot(x, z)
        for dz in Z_ORDER:
            send_block(it, own, zr.at[it, dz - 1], (x * ZS + wrap(z + dz, ZS), b))

    def send_x(it, dz):
        where = slot(x, wrap(z - dz, ZS))
        sems = x_own if dz == 0 else xr
        for dx in X_ORDER:
            if dz in X_FIRST[dx]:
                continue
            send_block(it, where, sems.at[it, dx - 1], (wrap(x + dx, XS) * ZS + z, b))

    def got_z(it, dz):
        wait_bytes(vbuf.at[it, slot(x, wrap(z - dz, ZS))], zr.at[it, dz - 1])
        send_x(it, dz)

    def got_own_x(it, dx):
        where = slot(wrap(x - dx, XS), z)
        wait_bytes(vbuf.at[it, where], x_own.at[it, dx - 1])
        for dz in X_FIRST[dx]:
            send_block(it, where, xr.at[it, dx - 1], (x * ZS + wrap(z + dz, ZS), b))

    def wait_x(it, dx):
        wait_bytes(vbuf.at[it, : (ZS - 1) * MODES], xr.at[it, dx - 1])

    def got_x(it, dx):
        wait_x(it, dx)
        coarse_row(it, -dx, False)

    def coarse_row(it, dx, first):
        span = pl.ds(pl.multiple_of(wrap(x + dx, XS) * (ZS * MODES), ZS * MODES), ZS * MODES)
        part = dot(cv[:, span], vbuf[it, span, :])
        if first:
            pacc[...] = part
        else:
            pacc[...] += part

    def residual_bands(it, group):
        for d in group:
            span = band(d)
            assembled = flux[span, :]
            if d < 8:
                if d in FACES:
                    f = FACES.index(d)
                    assembled += dot(sel_t[f], ebuf[it, band(f), :])
                else:
                    assembled += dot(selc_t[CORNERS.index(d)], ebuf[it, 512:, :])
            resid = (lv[span, :].astype(F32) - assembled).astype(BF)
            if it == ITERS - 1:
                out_resid[span, :] = resid
            moved = tr[span, :] + 0.25 * resid.astype(F32)
            tr[span, :] = moved
            x_ref[span, :128] = moved.astype(BF)

    for it in range(ITERS):
        last = it == ITERS - 1
        if it == 0:
            source = lambda span: flux[span, :].astype(BF)
            for j, piece in enumerate(select_from(source)):
                obuf[it, band(j), :] = piece.astype(BF)
            pl.semaphore_wait(barrier, len(greet))
            send_outgoing(it)

            s_copy(2).wait()
            s_tile(2, 512)

            build_basis()
            for f, d in enumerate(FACES):
                hb[:, band(f)] = dot(basis[:, band(d)], sel_t[f]).astype(BF)
            corner = dot(basis[:, band(CORNERS[0])], selc_t[0])
            for c in range(1, 4):
                corner += dot(basis[:, band(CORNERS[c])], selc_t[c])
            hb[:, 512:] = corner.astype(BF)
            cp_l.wait()
            rhs_of_flux()
        else:
            obuf[it] = (opart[...] + dot(wsel[...], cb[...])).astype(BF)
            send_outgoing(it)
            rhsp[...] -= dot(bw[...], cb[...])
            flux[...] += dot(wb[...], cb[...])
            tr[...] += dot(x_ref[:, 128:], cb[...])

        wait_bytes(ebuf.at[it, :REAL_OUT], ex_recv.at[it])
        rhs = rhsp[...] - dot(hb[...], ebuf[it])
        vbuf[it, slot(x, z), :] = rhs[:MODES].astype(BF)
        send_x(it, 0)
        send_z(it)

        jobs = [
            functools.partial(residual_bands, it, range(0, 6)),
            functools.partial(residual_bands, it, range(6, 12)),
        ]
        if not last:
            width, product = (256, s_tile_first) if it == 0 else (128, s_tile)
            jobs += [functools.partial(k_tile, i, width) for i in range(TILES)]
            jobs += [functools.partial(product, i) for i in range(TILES)]

            def finish(it=it):
                if it == 0:
                    for j, piece in enumerate(select_from(lambda span: wb[span, :])):
                        wsel[band(j), :] = piece.astype(BF)
                    bw[...] = dot(basis[...], wb[...]).astype(BF)
                source = lambda span: flux[span, :].astype(BF)
                for j, piece in enumerate(select_from(source)):
                    opart[band(j), :] = piece
                rhs_of_flux()

            jobs.append(finish)

        def work(n):
            for _ in range(min(n, len(jobs))):
                jobs.pop(0)()

        work(4)
        got_own_x(it, 1)
        got_own_x(it, 3)
        got_own_x(it, 2)
        got_z(it, 2)
        got_z(it, 6)
        got_z(it, 3)
        got_z(it, 5)
        got_z(it, 4)
        work(4 if it else 2)
        if it == 0:
            cp_c.wait()
        got_z(it, 1)
        got_z(it, 7)
        coarse_row(it, 0, True)
        got_x(it, 1)
        got_x(it, 3)
        got_x(it, 2)

        pbuf[it] = pacc[...].astype(BF)
        for dy, dc in ((2, 0), (2, 1), (1, 0), (3, 0), (1, 1), (3, 1), (0, 1)):
            to = 2 * wrap(y + dy, 4) + wrap(core + dc, 2)
            pltpu.make_async_remote_copy(
                src_ref=pbuf.at[it, rows(to, MODES)], dst_ref=rbuf.at[it, rows(2 * dy + dc, MODES)],
                send_sem=rs_send.at[it], recv_sem=rs_recv.at[it],
                device_id=(a, to), device_id_type=MESH,
            ).start()
        work(len(jobs))
        wait_bytes(rbuf.at[it, MODES:], rs_recv.at[it])
        total = pacc[rows(b, MODES), :]
        for j in range(1, COL):
            total += rbuf[it, j * MODES : (j + 1) * MODES, :].astype(F32)
        cb[:MODES, :] = total.astype(BF)

    out_trace[...] = (tr[...] + dot(x_ref[:, 128:], cb[...])).astype(BF)
    for it in range(ITERS):
        wait_bytes(obuf.at[it, :REAL_OUT], ex_send.at[it])
        wait_bytes(vbuf.at[it, : (SUB - 1) * MODES], ag_send.at[it])
        wait_bytes(pbuf.at[it, MODES:], rs_send.at[it])


def store_kernel(trace_ref, resid_ref, out_trace, out_resid, sem):
    first = pltpu.make_async_copy(trace_ref, out_trace.at[0, 0], sem.at[0])
    second = pltpu.make_async_copy(resid_ref, out_resid.at[0, 0], sem.at[1])
    first.start()
    second.start()
    first.wait()
    second.wait()


def local(trace_start, neumann_load, double_layer, single_inverse, interface_nodes, node_mode, mode_weight, coarse_inverse):
    hbm = pl.BlockSpec(memory_space=pl.ANY)
    vmem = pl.BlockSpec(memory_space=pltpu.VMEM)
    square = lambda: pltpu.VMEM((M, M), BF)
    tall = lambda kind: pltpu.VMEM((M, R), kind)
    dma = pltpu.SemaphoreType.DMA
    trace, resid = pl.pallas_call(
        kernel,
        out_shape=(pltpu.VMEM((M, R), BF), pltpu.VMEM((M, R), BF)),
        in_specs=[hbm, hbm, hbm, hbm, vmem, vmem, vmem, hbm],
        out_specs=(vmem, vmem),
        scratch_shapes=[
            tall(BF), tall(BF), square(), square(), pltpu.VMEM((512, 2048), BF),
            pltpu.VMEM((M, 256), BF), pltpu.VMEM((M, 256), BF), tall(F32), tall(F32), tall(BF),
            pltpu.VMEM((128, M), BF),
            pltpu.VMEM((4, 128, 128), BF), pltpu.VMEM((4, 128, 128), BF),
            pltpu.VMEM((4, 128, 128), BF), pltpu.VMEM((4, 128, 128), BF),
            pltpu.VMEM((128, ROWS_OUT), BF), pltpu.VMEM((ROWS_OUT, 128), BF), pltpu.VMEM((128, 128), BF),
            pltpu.VMEM((ROWS_OUT, R), F32), pltpu.VMEM((128, R), F32), pltpu.VMEM((128, R), BF),
            pltpu.VMEM((512, R), F32),
            pltpu.VMEM((ITERS, ROWS_OUT, R), BF), pltpu.VMEM((ITERS, ROWS_OUT, R), BF),
            pltpu.VMEM((ITERS, SUB * MODES, R), BF),
            pltpu.VMEM((ITERS, COL * MODES, R), BF), pltpu.VMEM((ITERS, COL * MODES, R), BF),
            dma((9,)),
            dma((ITERS,)), dma((ITERS,)), dma((ITERS,)), dma((ITERS, 7)), dma((ITERS, 3)), dma((ITERS, 3)),
            dma((ITERS,)), dma((ITERS,)),
        ],
        compiler_params=pltpu.CompilerParams(collective_id=0, has_side_effects=True),
    )(trace_start, neumann_load, double_layer, single_inverse, interface_nodes, node_mode, mode_weight, coarse_inverse)
    return pl.pallas_call(
        store_kernel,
        out_shape=(jax.ShapeDtypeStruct((1, 1, M, R), BF), jax.ShapeDtypeStruct((1, 1, M, R), BF)),
        in_specs=[hbm, hbm],
        out_specs=(hbm, hbm),
        scratch_shapes=[dma((2,))],
        compiler_params=pltpu.CompilerParams(vmem_limit_bytes=1 << 20),
    )(trace, resid)


def solution(mesh):
    four = P("sub", "col", None, None)
    three = P("sub", "col", None)
    return jax.shard_map(
        local,
        mesh=mesh,
        in_specs=(four, four, four, four, four, three, three, P("sub", "col")),
        out_specs=(four, four),
        check_vma=False,
    )
```
